32 devices in a mesh: groups: 2 (over y), aux: 4 (over z), pts: 2 (over x), rep: 2 (over core).
Axes of the slice: x: 2, y: 2, z: 4, core: 2. Of those that a mesh axis runs over, the one named last changes fastest.
Arguments:
- density_slab: bfloat16 [32, 1024, 1024], P('groups', 'aux', 'rep'), parts along dimension 0, may hold values from -0.005859375 to 0.005859375
- orbitals: bfloat16 [2048, 8192], P(('groups', 'rep'), 'pts'), parts along dimension 0, may hold values from -6 to 6
Outputs:
- rhs_share: float32 [16384, 8192], P(('groups', 'pts'), ('aux', 'rep')), parts along dimension 0
The draws below stay inside these ranges and needn't reach their ends.
There are 2 independent parts, one for each index of `groups`. The reference program is written for one: setup_inputs(seed, part) draws one part's arguments, and reference() takes and returns one part's arrays. A program takes and returns all parts, laid end to end along the dimension named above; each array names one. Nothing has to cross between parts.
All inputs are finite; a program needn't handle non-finite values.
Results may differ from the reference program's by a relative error of at most 0.0003.
Values may be sent and summed in bfloat16 or wider, within the bound.
A program may use at most 64 MiB of HBM per device.

```python
import jax
import jax.numpy as jnp
from jax import lax

NBF = 1024
NPTS = 8192
AUX = 16


def block_levels(own_key, extent, shards, smallest, largest):
    level = 1.0
    for dim, parts in shards:
        heights = jax.random.uniform(jax.random.fold_in(jax.random.fold_in(own_key, 6), dim), (parts,), jnp.float32, smallest / len(shards), largest / len(shards))
        level = level * jnp.repeat(jnp.exp(heights), extent[dim] // parts).reshape((-1,) + (1,) * (len(extent) - 1 - dim))
    return level


def noise(own_key, extent, deviation, limit, split=(), dtype=jnp.bfloat16):
    gain = block_levels(own_key, extent, split, -0.22, 0.18) if split else 1.0
    values = jax.random.normal(own_key, extent, jnp.float32) * deviation * gain
    return jnp.minimum(jnp.maximum(values, -limit), limit).astype(dtype)


def setup_inputs(seed: int = 0, part: int = 0) -> dict:
    seeds = jax.random.split(jax.random.key(seed), 3)
    part_splits = jax.random.split(jax.random.fold_in(seeds[2], part), 3)
    density_slab = noise(part_splits[0], (AUX, NBF, NBF), (NBF * NBF) ** -0.5, 0.005859375, ((1, 4), (2, 2)))
    orbitals = noise(part_splits[1], (NBF, NPTS), 1.0, 6.0, ((0, 2), (1, 2)))
    return dict(density_slab=density_slab, orbitals=orbitals)


def reference(density_slab, orbitals):
    colloc = orbitals.astype(jnp.float32)

    def one_slice(slab):
        contracted = jnp.dot(slab, orbitals, preferred_element_type=jnp.float32)
        return jnp.sum(colloc * contracted, axis=0)

    weights = lax.map(one_slice, density_slab)
    total = jnp.dot(weights.T, weights, precision=lax.Precision.HIGHEST, preferred_element_type=jnp.float32)
    return total / jnp.float32(AUX)
```

```python
import functools

import jax
import jax.numpy as jnp
from jax import lax
from jax.experimental import pallas as pl
from jax.experimental.pallas import tpu as pltpu
from jax.sharding import PartitionSpec as P


def weights_kernel(group, d_ref, q_ref, p_ref, w_ref):
    n_k, n_p, n_q = d_ref.shape
    q_rows = q_ref[...]
    p_rows = p_ref[...].astype(jnp.float32)
    for k in range(0, n_k, group):
        lhs = d_ref[k : k + group].reshape(group * n_p, n_q)
        c = jnp.dot(lhs, q_rows, preferred_element_type=jnp.float32)
        for j in range(group):
            part = c[j * n_p : (j + 1) * n_p] * p_rows
            w_ref[k + j : k + j + 1, :] = jnp.sum(part, axis=0, keepdims=True)


def partial_weights(density, q_rows, p_rows, tile=512, group=4):
    n_k, n_p, n_q = density.shape
    n_pts = q_rows.shape[1]
    tile = min(tile, n_pts)
    return pl.pallas_call(
        functools.partial(weights_kernel, group),
        grid=(n_pts // tile,),
        in_specs=[
            pl.BlockSpec((n_k, n_p, n_q), lambda i: (0, 0, 0), pipeline_mode=pl.Buffered(1)),
            pl.BlockSpec((n_q, tile), lambda i: (0, i)),
            pl.BlockSpec((n_p, tile), lambda i: (0, i)),
        ],
        out_specs=pl.BlockSpec((n_k, tile), lambda i: (0, i)),
        out_shape=jax.ShapeDtypeStruct((n_k, n_pts), jnp.float32),
        compiler_params=pltpu.CompilerParams(vmem_limit_bytes=48 << 20),
        cost_estimate=pl.CostEstimate(
            flops=2 * n_k * n_p * n_q * n_pts,
            bytes_accessed=2 * (n_k * n_p * n_q + (n_p + n_q) * n_pts),
            transcendentals=0,
        ),
    )(density, q_rows, p_rows)


def split(w):
    high = w.astype(jnp.bfloat16)
    return high, (w - high.astype(jnp.float32)).astype(jnp.bfloat16)


def outer_kernel(scale, row_ref, col_ref, o_ref):
    r_hi, r_lo = split(row_ref[...])
    c_hi, c_lo = split(col_ref[...])
    left = jnp.concatenate([r_hi, r_hi, r_lo], axis=0)
    right = jnp.concatenate([c_hi, c_lo, c_hi], axis=0)
    o_ref[...] = (
        lax.dot_general(
            left, right, (((0,), (0,)), ((), ())), preferred_element_type=jnp.float32
        )
        * scale
    )


def outer(row_w, col_w, tile=512):
    n_k, n_rows = row_w.shape
    n_cols = col_w.shape[1]
    tile = min(tile, n_rows)
    return pl.pallas_call(
        functools.partial(outer_kernel, 1.0 / n_k),
        grid=(n_rows // tile,),
        in_specs=[
            pl.BlockSpec((n_k, tile), lambda i: (0, i)),
            pl.BlockSpec((n_k, n_cols), lambda i: (0, 0)),
        ],
        out_specs=pl.BlockSpec((tile, n_cols), lambda i: (i, 0)),
        out_shape=jax.ShapeDtypeStruct((n_rows, n_cols), jnp.float32),
        compiler_params=pltpu.CompilerParams(vmem_limit_bytes=32 << 20),
    )(row_w, col_w)


def per_device(density_slab, orbitals):
    aux_index = lax.axis_index("aux")
    rep_index = lax.axis_index("rep")
    n_aux = lax.axis_size("aux")
    n_rep = lax.axis_size("rep")
    n_p = density_slab.shape[1]
    first = aux_index * n_p
    owner = first // orbitals.shape[0]
    ship = lax.dynamic_slice_in_dim(orbitals, first % orbitals.shape[0], n_p, 0)
    both = lax.all_gather(ship, "rep", axis=0)
    p_rows = lax.dynamic_index_in_dim(both, owner, 0, keepdims=False)
    own_w = lax.psum(partial_weights(density_slab, orbitals, p_rows), ("aux", "rep"))
    all_w = lax.all_gather(own_w, "pts", axis=1, tiled=True)
    col_width = all_w.shape[1] // (n_aux * n_rep)
    column_w = lax.dynamic_slice_in_dim(
        all_w, (aux_index * n_rep + rep_index) * col_width, col_width, 1
    )
    return outer(own_w, column_w)


def solution(mesh):
    return jax.shard_map(
        per_device,
        mesh=mesh,
        in_specs=(P("groups", "aux", "rep"), P(("groups", "rep"), "pts")),
        out_specs=P(("groups", "pts"), ("aux", "rep")),
        check_vma=False,
    )
```

```python
import functools

import jax
import jax.numpy as jnp
from jax import lax
from jax.experimental import pallas as pl
from jax.experimental.pallas import tpu as pltpu
from jax.sharding import PartitionSpec as P


MESH = pl.DeviceIdType.MESH


def split(w):
    high = w.astype(jnp.bfloat16)
    return high, (w - high.astype(jnp.float32)).astype(jnp.bfloat16)


def share_kernel(
    sizes, d_hbm, orb_hbm, left_ref, right_ref,
    d_buf, q_buf, p_buf, part, rs_buf, ag_buf, col_buf, flat, col_flat,
    d_sem, q_sem, p_sem, ps_sem, rs_send, rs_recv, ag_send, ag_recv, col_send, col_recv,
):
    n_aux, n_pts, n_rep, group, tile = sizes
    n_k, n_p, n_q = d_hbm.shape
    members = n_aux * n_rep
    chunks, _, rows, width = part.shape
    a, x, r = lax.axis_index("aux"), lax.axis_index("pts"), lax.axis_index("rep")
    me = a * n_rep + r
    home = me // chunks
    first = a * n_p
    owner, offset = first // n_q, pl.multiple_of(first % n_q, n_p)

    def member(j):
        return {"aux": j // n_rep, "rep": j % n_rep}

    def cols(g):
        return pl.ds(pl.multiple_of(g * width, width), width)

    def d_copy(i):
        ks = pl.ds(i * group, group)
        return pltpu.make_async_copy(d_hbm.at[ks], d_buf.at[ks], d_sem.at[i])

    def q_copy(g):
        return pltpu.make_async_copy(orb_hbm.at[:, cols(g)], q_buf.at[g], q_sem.at[g])

    def p_local(g):
        return pltpu.make_async_copy(
            orb_hbm.at[pl.ds(offset, n_p), cols(g)], p_buf.at[g], p_sem.at[g]
        )

    def p_remote(g, step):
        return pltpu.make_async_remote_copy(
            orb_hbm.at[pl.ds(offset, n_p), cols(g)], p_buf.at[g],
            ps_sem.at[g, step - 1], p_sem.at[g],
            device_id={"rep": (r + step) % n_rep}, device_id_type=MESH,
        )

    def rs_copy(g, step):
        j = (me + step) % members
        return pltpu.make_async_remote_copy(
            part.at[g, j], rs_buf.at[g, step - 1],
            rs_send.at[g, step - 1], rs_recv.at[g, step - 1],
            device_id=member(j), device_id_type=MESH,
        )

    def ag_copy(g, step):
        return pltpu.make_async_remote_copy(
            ag_buf.at[g, me], ag_buf.at[g, me],
            ag_send.at[g, step - 1], ag_recv.at[g, step - 1],
            device_id=member((me + step) % members), device_id_type=MESH,
        )

    def ag_arrival(g, step):
        source = (me + members - step) % members
        return pltpu.make_async_remote_copy(
            ag_buf.at[g, source], ag_buf.at[g, source],
            ag_send.at[g, step - 1], ag_recv.at[g, step - 1],
            device_id=member((me + step) % members), device_id_type=MESH,
        )

    def col_copy(g, step):
        target = member(x * chunks + g)
        target["pts"] = (x + step) % n_pts
        return pltpu.make_async_remote_copy(
            ag_buf.at[g, me], col_buf.at[me],
            col_send.at[g, step - 1], col_recv.at[me],
            device_id=target, device_id_type=MESH,
        )

    def col_arrival(i):
        return pltpu.make_async_remote_copy(
            ag_buf.at[0, i], col_buf.at[i], col_send.at[0, 0], col_recv.at[i],
            device_id={"pts": home}, device_id_type=MESH,
        )

    q_copy(0).start()
    for i in range(n_k // group):
        d_copy(i).start()
    for g in range(1, chunks):
        q_copy(g).start()

    barrier = pltpu.get_barrier_semaphore()
    for step in range(1, members):
        pl.semaphore_signal(
            barrier, inc=1, device_id=member((me + step) % members), device_id_type=MESH
        )

    @pl.when(home != x)
    def _():
        for i in range(members):
            source = {"aux": i // n_rep, "rep": i % n_rep, "pts": home}
            pl.semaphore_signal(barrier, inc=1, device_id=source, device_id_type=MESH)

    @pl.when(owner == r)
    def _():
        for g in range(chunks):
            p_local(g).start()

    pl.semaphore_wait(barrier, members - 1 + (n_pts - 1) * chunks)

    @pl.when(owner == r)
    def _():
        for g in range(chunks):
            for step in range(1, n_rep):
                p_remote(g, step).start()

    def finish(g):
        for step in range(1, members):
            rs_copy(g, step).wait_recv()
        total = part[g, me]
        for step in range(1, members):
            total = total + rs_buf[g, step - 1]
        ag_buf[g, me] = total
        for step in range(1, members):
            ag_copy(g, step).start()
        for step in range(1, n_pts):
            col_copy(g, step).start()

    def chunk(g, carry):
        q_copy(g).wait()

        @pl.when(g == 0)
        def _():
            for i in range(n_k // group):
                d_copy(i).wait()

        @pl.when(owner == r)
        def _():
            p_local(g).wait()

        @pl.when(owner != r)
        def _():
            p_remote(g, 1).wait_recv()

        for t in range(0, width, tile):
            q_rows = q_buf[g, :, t : t + tile]
            p_rows = p_buf[g, :, t : t + tile].astype(jnp.float32)
            for k in range(0, n_k, group):
                lhs = d_buf[k : k + group].reshape(group * n_p, n_q)
                c = jnp.dot(lhs, q_rows, preferred_element_type=jnp.float32)
                for j in range(group):
                    term = c[j * n_p : (j + 1) * n_p] * p_rows
                    row = (k + j) % rows
                    part[g, (k + j) // rows, row : row + 1, t : t + tile] = jnp.sum(
                        term, axis=0, keepdims=True
                    )
        for step in range(1, members):
            rs_copy(g, step).start()

        @pl.when(g > 0)
        def _():
            finish(g - 1)

        return carry

    lax.fori_loop(0, chunks, chunk, 0)
    finish(chunks - 1)

    for g in range(chunks):
        for step in range(1, members):
            ag_arrival(g, step).wait_recv()
        for i in range(members):
            flat[i * rows : (i + 1) * rows, :] = ag_buf[g, i]
        high, low = split(flat[...])
        there = slice(g * width, (g + 1) * width)
        left_ref[0:n_k, there] = high
        left_ref[n_k : 2 * n_k, there] = high
        left_ref[2 * n_k : 3 * n_k, there] = low

    @pl.when(home == x)
    def _():
        for i in range(members):
            col_flat[i * rows : (i + 1) * rows, :] = ag_buf[me % chunks, i]

    @pl.when(home != x)
    def _():
        for i in range(members):
            col_arrival(i).wait_recv()
            col_flat[i * rows : (i + 1) * rows, :] = col_buf[i]

    high, low = split(col_flat[...])
    right_ref[0:n_k, :] = high
    right_ref[n_k : 2 * n_k, :] = low
    right_ref[2 * n_k : 3 * n_k, :] = high

    for g in range(chunks):
        for step in range(1, members):
            rs_copy(g, step).wait_send()
            ag_copy(g, step).wait_send()
        for step in range(1, n_pts):
            col_copy(g, step).wait_send()

    @pl.when(owner == r)
    def _():
        for g in range(chunks):
            for step in range(1, n_rep):
                p_remote(g, step).wait_send()


def factors(density, orbitals, group=4, tile=512):
    n_k, n_p, n_q = density.shape
    own_pts = orbitals.shape[1]
    n_aux, n_pts, n_rep = (lax.axis_size(name) for name in ("aux", "pts", "rep"))
    members = n_aux * n_rep
    chunks = members // n_pts
    width = own_pts // chunks
    rows = n_k // members
    dma = pltpu.SemaphoreType.DMA
    f32, bf16 = jnp.float32, jnp.bfloat16
    return pl.pallas_call(
        functools.partial(share_kernel, (n_aux, n_pts, n_rep, group, min(tile, width))),
        in_specs=[pl.BlockSpec(memory_space=pl.ANY)] * 2,
        out_specs=[pl.BlockSpec(memory_space=pltpu.VMEM)] * 2,
        out_shape=[
            jax.ShapeDtypeStruct((3 * n_k, own_pts), bf16),
            jax.ShapeDtypeStruct((3 * n_k, width), bf16),
        ],
        scratch_shapes=[
            pltpu.VMEM((n_k, n_p, n_q), bf16),
            pltpu.VMEM((chunks, n_q, width), bf16),
            pltpu.VMEM((chunks, n_p, width), bf16),
            pltpu.VMEM((chunks, members, rows, width), f32),
            pltpu.VMEM((chunks, members - 1, rows, width), f32),
            pltpu.VMEM((chunks, members, rows, width), f32),
            pltpu.VMEM((members, rows, width), f32),
            pltpu.VMEM((n_k, width), f32),
            pltpu.VMEM((n_k, width), f32),
            dma((n_k // group,)),
            dma((chunks,)),
            dma((chunks,)),
            dma((chunks, n_rep - 1)),
            dma((chunks, members - 1)),
            dma((chunks, members - 1)),
            dma((chunks, members - 1)),
            dma((chunks, members - 1)),
            dma((chunks, n_pts - 1)),
            dma((members,)),
        ],
        compiler_params=pltpu.CompilerParams(
            collective_id=0, has_side_effects=True, vmem_limit_bytes=48 << 20
        ),
        cost_estimate=pl.CostEstimate(
            flops=2 * n_k * n_p * n_q * own_pts,
            bytes_accessed=2 * (n_k * n_p * n_q + (n_p + n_q) * own_pts),
            transcendentals=0,
        ),
    )(density, orbitals)


def outer_kernel(scale, left_ref, right_ref, o_ref):
    o_ref[...] = (
        lax.dot_general(
            left_ref[...], right_ref[...], (((0,), (0,)), ((), ())),
            preferred_element_type=jnp.float32,
        )
        * scale
    )


def outer(left, right, scale, tile=512):
    depth, n_rows = left.shape
    n_cols = right.shape[1]
    tile = min(tile, n_rows)
    return pl.pallas_call(
        functools.partial(outer_kernel, scale),
        grid=(n_rows // tile,),
        in_specs=[
            pl.BlockSpec((depth, tile), lambda i: (0, i)),
            pl.BlockSpec((depth, n_cols), lambda i: (0, 0)),
        ],
        out_specs=pl.BlockSpec((tile, n_cols), lambda i: (i, 0)),
        out_shape=jax.ShapeDtypeStruct((n_rows, n_cols), jnp.float32),
        compiler_params=pltpu.CompilerParams(vmem_limit_bytes=32 << 20),
    )(left, right)


def per_device(density_slab, orbitals):
    left, right = factors(density_slab, orbitals)
    return outer(left, right, 1.0 / density_slab.shape[0])


def solution(mesh):
    return jax.shard_map(
        per_device,
        mesh=mesh,
        in_specs=(P("groups", "aux", "rep"), P(("groups", "rep"), "pts")),
        out_specs=P(("groups", "pts"), ("aux", "rep")),
        check_vma=False,
    )
```

```python
import functools

import jax
import jax.numpy as jnp
from jax import lax
from jax.experimental import pallas as pl
from jax.experimental.pallas import tpu as pltpu
from jax.sharding import PartitionSpec as P


MESH = pl.DeviceIdType.MESH


def split(w):
    high = w.astype(jnp.bfloat16)
    return high, (w - high.astype(jnp.float32)).astype(jnp.bfloat16)


def share_kernel(
    sizes, d_hbm, orb_hbm, left_ref, right_ref,
    d_buf, q_buf, p_buf, part, rs_buf, ag_buf, col_buf, flat, col_flat,
    d_sem, q_sem, p_sem, ps_sem, rs_send, rs_recv, ag_send, ag_recv, col_send, col_recv,
):
    n_aux, n_pts, n_rep, group, tile = sizes
    n_k, n_p, n_q = d_hbm.shape
    members = n_aux * n_rep
    chunks, _, rows, width = part.shape
    a, x, r = lax.axis_index("aux"), lax.axis_index("pts"), lax.axis_index("rep")
    me = a * n_rep + r
    home = me // chunks
    first = a * n_p
    owner, offset = first // n_q, pl.multiple_of(first % n_q, n_p)

    def member(j):
        return {"aux": j // n_rep, "rep": j % n_rep}

    def cols(g):
        return pl.ds(pl.multiple_of(g * width, width), width)

    def d_copy(i):
        ks = pl.ds(i * group, group)
        return pltpu.make_async_copy(d_hbm.at[ks], d_buf.at[ks], d_sem.at[i])

    def q_copy(g):
        return pltpu.make_async_copy(orb_hbm.at[:, cols(g)], q_buf.at[g], q_sem.at[g])

    def p_local(g):
        return pltpu.make_async_copy(
            orb_hbm.at[pl.ds(offset, n_p), cols(g)], p_buf.at[g], p_sem.at[g]
        )

    def p_remote(g, step):
        return pltpu.make_async_remote_copy(
            orb_hbm.at[pl.ds(offset, n_p), cols(g)], p_buf.at[g],
            ps_sem.at[g, step - 1], p_sem.at[g],
            device_id={"rep": (r + step) % n_rep}, device_id_type=MESH,
        )

    def rs_copy(g, step):
        j = (me + step) % members
        return pltpu.make_async_remote_copy(
            part.at[g, j], rs_buf.at[g, step - 1],
            rs_send.at[g, step - 1], rs_recv.at[g, step - 1],
            device_id=member(j), device_id_type=MESH,
        )

    def ag_copy(g, step):
        return pltpu.make_async_remote_copy(
            ag_buf.at[g, me], ag_buf.at[g, me],
            ag_send.at[g, step - 1], ag_recv.at[g, step - 1],
            device_id=member((me + step) % members), device_id_type=MESH,
        )

    def ag_arrival(g, step):
        source = (me + members - step) % members
        return pltpu.make_async_remote_copy(
            ag_buf.at[g, source], ag_buf.at[g, source],
            ag_send.at[g, step - 1], ag_recv.at[g, step - 1],
            device_id=member((me + step) % members), device_id_type=MESH,
        )

    def col_copy(g, step):
        target = member(x * chunks + g)
        target["pts"] = (x + step) % n_pts
        return pltpu.make_async_remote_copy(
            ag_buf.at[g, me], col_buf.at[me],
            col_send.at[g, step - 1], col_recv.at[me],
            device_id=target, device_id_type=MESH,
        )

    def col_arrival(i):
        return pltpu.make_async_remote_copy(
            ag_buf.at[0, i], col_buf.at[i], col_send.at[0, 0], col_recv.at[i],
            device_id={"pts": home}, device_id_type=MESH,
        )

    q_copy(0).start()
    for i in range(n_k // group):
        d_copy(i).start()
    for g in range(1, chunks):
        q_copy(g).start()

    barrier = pltpu.get_barrier_semaphore()
    for step in range(1, members):
        pl.semaphore_signal(
            barrier, inc=1, device_id=member((me + step) % members), device_id_type=MESH
        )

    @pl.when(home != x)
    def _():
        for i in range(members):
            source = {"aux": i // n_rep, "rep": i % n_rep, "pts": home}
            pl.semaphore_signal(barrier, inc=1, device_id=source, device_id_type=MESH)

    @pl.when(owner == r)
    def _():
        for g in range(chunks):
            p_local(g).start()

    pl.semaphore_wait(barrier, members - 1 + (n_pts - 1) * chunks)

    @pl.when(owner == r)
    def _():
        for g in range(chunks):
            for step in range(1, n_rep):
                p_remote(g, step).start()

    def finish(g):
        for step in range(1, members):
            rs_copy(g, step).wait_recv()
        total = part[g, me]
        for step in range(1, members):
            total = total + rs_buf[g, step - 1]
        ag_buf[g, me] = total
        for step in range(1, members):
            ag_copy(g, step).start()
        for step in range(1, n_pts):
            col_copy(g, step).start()

    def chunk(g, carry):
        q_copy(g).wait()

        @pl.when(g == 0)
        def _():
            for i in range(n_k // group):
                d_copy(i).wait()

        @pl.when(owner == r)
        def _():
            p_local(g).wait()

        @pl.when(owner != r)
        def _():
            p_remote(g, 1).wait_recv()

        for t in range(0, width, tile):
            q_rows = q_buf[g, :, t : t + tile]
            p_rows = p_buf[g, :, t : t + tile].astype(jnp.float32)
            for k in range(0, n_k, group):
                lhs = d_buf[k : k + group].reshape(group * n_p, n_q)
                c = jnp.dot(lhs, q_rows, preferred_element_type=jnp.float32)
                for j in range(group):
                    term = c[j * n_p : (j + 1) * n_p] * p_rows
                    row = (k + j) % rows
                    part[g, (k + j) // rows, row : row + 1, t : t + tile] = jnp.sum(
                        term, axis=0, keepdims=True
                    )
        for step in range(1, members):
            rs_copy(g, step).start()

        @pl.when(g > 0)
        def _():
            finish(g - 1)

        return carry

    lax.fori_loop(0, chunks, chunk, 0)
    finish(chunks - 1)

    for g in range(chunks):
        for step in range(1, members):
            ag_arrival(g, step).wait_recv()
        for i in range(members):
            flat[i * rows : (i + 1) * rows, :] = ag_buf[g, i]
        high, low = split(flat[...])
        there = slice(g * width, (g + 1) * width)
        left_ref[0:n_k, there] = high
        left_ref[n_k : 2 * n_k, there] = high
        left_ref[2 * n_k : 3 * n_k, there] = low

    @pl.when(home == x)
    def _():
        for i in range(members):
            col_flat[i * rows : (i + 1) * rows, :] = ag_buf[me % chunks, i]

    @pl.when(home != x)
    def _():
        for i in range(members):
            col_arrival(i).wait_recv()
            col_flat[i * rows : (i + 1) * rows, :] = col_buf[i]

    high, low = split(col_flat[...])
    right_ref[0:n_k, :] = high
    right_ref[n_k : 2 * n_k, :] = low
    right_ref[2 * n_k : 3 * n_k, :] = high

    for g in range(chunks):
        for step in range(1, members):
            rs_copy(g, step).wait_send()
            ag_copy(g, step).wait_send()
        for step in range(1, n_pts):
            col_copy(g, step).wait_send()

    @pl.when(owner == r)
    def _():
        for g in range(chunks):
            for step in range(1, n_rep):
                p_remote(g, step).wait_send()


def factors(density, orbitals, group=4, tile=512):
    n_k, n_p, n_q = density.shape
    own_pts = orbitals.shape[1]
    n_aux, n_pts, n_rep = (lax.axis_size(name) for name in ("aux", "pts", "rep"))
    members = n_aux * n_rep
    chunks = members // n_pts
    width = own_pts // chunks
    rows = n_k // members
    dma = pltpu.SemaphoreType.DMA
    f32, bf16 = jnp.float32, jnp.bfloat16
    return pl.pallas_call(
        functools.partial(share_kernel, (n_aux, n_pts, n_rep, group, min(tile, width))),
        in_specs=[pl.BlockSpec(memory_space=pl.ANY)] * 2,
        out_specs=[pl.BlockSpec(memory_space=pltpu.VMEM)] * 2,
        out_shape=[
            jax.ShapeDtypeStruct((3 * n_k, own_pts), bf16),
            jax.ShapeDtypeStruct((3 * n_k, width), bf16),
        ],
        scratch_shapes=[
            pltpu.VMEM((n_k, n_p, n_q), bf16),
            pltpu.VMEM((chunks, n_q, width), bf16),
            pltpu.VMEM((chunks, n_p, width), bf16),
            pltpu.VMEM((chunks, members, rows, width), f32),
            pltpu.VMEM((chunks, members - 1, rows, width), f32),
            pltpu.VMEM((chunks, members, rows, width), f32),
            pltpu.VMEM((members, rows, width), f32),
            pltpu.VMEM((n_k, width), f32),
            pltpu.VMEM((n_k, width), f32),
            dma((n_k // group,)),
            dma((chunks,)),
            dma((chunks,)),
            dma((chunks, n_rep - 1)),
            dma((chunks, members - 1)),
            dma((chunks, members - 1)),
            dma((chunks, members - 1)),
            dma((chunks, members - 1)),
            dma((chunks, n_pts - 1)),
            dma((members,)),
        ],
        compiler_params=pltpu.CompilerParams(
            collective_id=0, has_side_effects=True, vmem_limit_bytes=60 << 20
        ),
        cost_estimate=pl.CostEstimate(
            flops=2 * n_k * n_p * n_q * own_pts,
            bytes_accessed=2 * (n_k * n_p * n_q + (n_p + n_q) * own_pts),
            transcendentals=0,
        ),
    )(density, orbitals)


def outer_kernel(
    scale, tile, slots, left_hbm, right_hbm, o_ref, left, right, buf, in_sem, sem
):
    steps = o_ref.shape[0] // tile
    parts = in_sem.shape[0] - 1
    width = o_ref.shape[0] // parts

    def fetch(g):
        there = pl.ds(g * width, width)
        return pltpu.make_async_copy(left_hbm.at[:, there], left.at[:, there], in_sem.at[g])

    def store(i):
        return pltpu.make_async_copy(
            buf.at[i % slots], o_ref.at[pl.ds(i * tile, tile)], sem.at[i % slots]
        )

    whole = pltpu.make_async_copy(right_hbm, right, in_sem.at[parts])
    whole.start()
    for g in range(parts):
        fetch(g).start()
    whole.wait()
    for i in range(steps):
        if i * tile % width == 0:
            fetch(i * tile // width).wait()
        if i >= slots:
            store(i - slots).wait()
        buf[i % slots] = (
            lax.dot_general(
                left[:, i * tile : (i + 1) * tile], right[...],
                (((0,), (0,)), ((), ())), preferred_element_type=jnp.float32,
            )
            * scale
        )
        store(i).start()
    for i in range(max(0, steps - slots), steps):
        store(i).wait()


def outer(left, right, scale, tile=256, slots=4, parts=4):
    n_rows, n_cols = left.shape[1], right.shape[1]
    tile = min(tile, n_rows // parts)
    return pl.pallas_call(
        functools.partial(outer_kernel, scale, tile, slots),
        in_specs=[pl.BlockSpec(memory_space=pl.ANY)] * 2,
        out_specs=pl.BlockSpec(memory_space=pl.ANY),
        out_shape=jax.ShapeDtypeStruct((n_rows, n_cols), jnp.float32),
        scratch_shapes=[
            pltpu.VMEM(left.shape, left.dtype),
            pltpu.VMEM(right.shape, right.dtype),
            pltpu.VMEM((slots, tile, n_cols), jnp.float32),
            pltpu.SemaphoreType.DMA((parts + 1,)),
            pltpu.SemaphoreType.DMA((slots,)),
        ],
        compiler_params=pltpu.CompilerParams(vmem_limit_bytes=62 << 20),
    )(left, right)


def per_device(density_slab, orbitals):
    left, right = factors(density_slab, orbitals)
    return outer(left, right, 1.0 / density_slab.shape[0])


def solution(mesh):
    return jax.shard_map(
        per_device,
        mesh=mesh,
        in_specs=(P("groups", "aux", "rep"), P(("groups", "rep"), "pts")),
        out_specs=P(("groups", "pts"), ("aux", "rep")),
        check_vma=False,
    )
```

```python
import functools

import jax
import jax.numpy as jnp
from jax import lax
from jax.experimental import pallas as pl
from jax.experimental.pallas import tpu as pltpu
from jax.sharding import PartitionSpec as P


MESH = pl.DeviceIdType.MESH


def split(w):
    high = w.astype(jnp.bfloat16)
    return high, (w - high.astype(jnp.float32)).astype(jnp.bfloat16)


def share_kernel(
    sizes, d_hbm, orb_hbm, left_ref, right_ref,
    d_buf, q_buf, p_buf, part, rs_buf, ag_buf, col_buf, flat, col_flat,
    d_sem, q_sem, p_sem, ps_sem, rs_send, rs_recv, ag_send, ag_recv, col_send, col_recv,
):
    n_aux, n_pts, n_rep, group, tile = sizes
    n_k, n_p, n_q = d_hbm.shape
    members = n_aux * n_rep
    chunks, _, rows, width = part.shape
    a, x, r = lax.axis_index("aux"), lax.axis_index("pts"), lax.axis_index("rep")
    me = a * n_rep + r
    home = me // chunks
    first = a * n_p
    owner, offset = first // n_q, pl.multiple_of(first % n_q, n_p)

    def member(j):
        return {"aux": j // n_rep, "rep": j % n_rep}

    def cols(g):
        return pl.ds(pl.multiple_of(g * width, width), width)

    def d_copy(i):
        ks = pl.ds(i * group, group)
        return pltpu.make_async_copy(d_hbm.at[ks], d_buf.at[ks], d_sem.at[i])

    def q_copy(g):
        return pltpu.make_async_copy(orb_hbm.at[:, cols(g)], q_buf.at[g], q_sem.at[g])

    def p_local(g):
        return pltpu.make_async_copy(
            orb_hbm.at[pl.ds(offset, n_p), cols(g)], p_buf.at[g], p_sem.at[g]
        )

    def p_remote(g, step):
        return pltpu.make_async_remote_copy(
            orb_hbm.at[pl.ds(offset, n_p), cols(g)], p_buf.at[g],
            ps_sem.at[g, step - 1], p_sem.at[g],
            device_id={"rep": (r + step) % n_rep}, device_id_type=MESH,
        )

    def rs_copy(g, step):
        j = (me + step) % members
        return pltpu.make_async_remote_copy(
            part.at[g, j], rs_buf.at[g, step - 1],
            rs_send.at[g, step - 1], rs_recv.at[g, step - 1],
            device_id=member(j), device_id_type=MESH,
        )

    def ag_copy(g, step):
        return pltpu.make_async_remote_copy(
            ag_buf.at[g, me], ag_buf.at[g, me],
            ag_send.at[g, step - 1], ag_recv.at[g, step - 1],
            device_id=member((me + step) % members), device_id_type=MESH,
        )

    def ag_arrival(g, step):
        source = (me + members - step) % members
        return pltpu.make_async_remote_copy(
            ag_buf.at[g, source], ag_buf.at[g, source],
            ag_send.at[g, step - 1], ag_recv.at[g, step - 1],
            device_id=member((me + step) % members), device_id_type=MESH,
        )

    def col_copy(g, step):
        target = member(x * chunks + g)
        target["pts"] = (x + step) % n_pts
        return pltpu.make_async_remote_copy(
            ag_buf.at[g, me], col_buf.at[me],
            col_send.at[g, step - 1], col_recv.at[me],
            device_id=target, device_id_type=MESH,
        )

    def col_arrival(i):
        return pltpu.make_async_remote_copy(
            ag_buf.at[0, i], col_buf.at[i], col_send.at[0, 0], col_recv.at[i],
            device_id={"pts": home}, device_id_type=MESH,
        )

    d_copy(0).start()
    q_copy(0).start()
    for i in range(1, n_k // group):
        d_copy(i).start()
    for g in range(1, chunks):
        q_copy(g).start()

    barrier = pltpu.get_barrier_semaphore()
    for step in range(1, members):
        pl.semaphore_signal(
            barrier, inc=1, device_id=member((me + step) % members), device_id_type=MESH
        )

    @pl.when(home != x)
    def _():
        for i in range(members):
            source = {"aux": i // n_rep, "rep": i % n_rep, "pts": home}
            pl.semaphore_signal(barrier, inc=1, device_id=source, device_id_type=MESH)

    @pl.when(owner == r)
    def _():
        for g in range(chunks):
            p_local(g).start()

    pl.semaphore_wait(barrier, members - 1 + (n_pts - 1) * chunks)

    @pl.when(owner == r)
    def _():
        for g in range(chunks):
            for step in range(1, n_rep):
                p_remote(g, step).start()

    def finish(g):
        for step in range(1, members):
            rs_copy(g, step).wait_recv()
        total = part[g, me]
        for step in range(1, members):
            total = total + rs_buf[g, step - 1]
        ag_buf[g, me] = total
        for step in range(1, members):
            ag_copy(g, step).start()
        for step in range(1, n_pts):
            col_copy(g, step).start()

    def chunk(g, opening):
        q_copy(g).wait()

        @pl.when(owner == r)
        def _():
            p_local(g).wait()

        @pl.when(owner != r)
        def _():
            p_remote(g, 1).wait_recv()

        for t in range(0, width, tile):
            q_rows = q_buf[g, :, t : t + tile]
            p_rows = p_buf[g, :, t : t + tile].astype(jnp.float32)
            for k in range(0, n_k, group):
                if opening and t == 0:
                    d_copy(k // group).wait()
                lhs = d_buf[k : k + group].reshape(group * n_p, n_q)
                c = jnp.dot(lhs, q_rows, preferred_element_type=jnp.float32)
                for j in range(group):
                    term = c[j * n_p : (j + 1) * n_p] * p_rows
                    row = (k + j) % rows
                    part[g, (k + j) // rows, row : row + 1, t : t + tile] = jnp.sum(
                        term, axis=0, keepdims=True
                    )
            if t == 0 and not opening:
                finish(g - 1)
        for step in range(1, members):
            rs_copy(g, step).start()

    def assemble(g):
        for step in range(1, members):
            ag_arrival(g, step).wait_recv()
        for i in range(members):
            flat[i * rows : (i + 1) * rows, :] = ag_buf[g, i]
        high, low = split(flat[...])
        there = slice(g * width, (g + 1) * width)
        left_ref[0:n_k, there] = high
        left_ref[n_k : 2 * n_k, there] = high
        left_ref[2 * n_k : 3 * n_k, there] = low

    def drain(g):
        for step in range(1, members):
            rs_copy(g, step).wait_send()
            ag_copy(g, step).wait_send()
        for step in range(1, n_pts):
            col_copy(g, step).wait_send()

    chunk(0, True)

    def later(g, carry):
        chunk(g, False)
        return carry

    lax.fori_loop(1, chunks, later, 0)
    for g in range(chunks - 1):
        assemble(g)
        drain(g)

    @pl.when(owner == r)
    def _():
        for g in range(chunks):
            for step in range(1, n_rep):
                p_remote(g, step).wait_send()

    finish(chunks - 1)
    assemble(chunks - 1)

    @pl.when(home == x)
    def _():
        for i in range(members):
            col_flat[i * rows : (i + 1) * rows, :] = ag_buf[me % chunks, i]

    @pl.when(home != x)
    def _():
        for i in range(members):
            col_arrival(i).wait_recv()
            col_flat[i * rows : (i + 1) * rows, :] = col_buf[i]

    high, low = split(col_flat[...])
    right_ref[0:n_k, :] = high
    right_ref[n_k : 2 * n_k, :] = low
    right_ref[2 * n_k : 3 * n_k, :] = high
    drain(chunks - 1)


def factors(density, orbitals, group=4, tile=512):
    n_k, n_p, n_q = density.shape
    own_pts = orbitals.shape[1]
    n_aux, n_pts, n_rep = (lax.axis_size(name) for name in ("aux", "pts", "rep"))
    members = n_aux * n_rep
    chunks = members // n_pts
    width = own_pts // chunks
    rows = n_k // members
    dma = pltpu.SemaphoreType.DMA
    f32, bf16 = jnp.float32, jnp.bfloat16
    return pl.pallas_call(
        functools.partial(share_kernel, (n_aux, n_pts, n_rep, group, min(tile, width))),
        in_specs=[pl.BlockSpec(memory_space=pl.ANY)] * 2,
        out_specs=[pl.BlockSpec(memory_space=pltpu.VMEM)] * 2,
        out_shape=[
            jax.ShapeDtypeStruct((3 * n_k, own_pts), bf16),
            jax.ShapeDtypeStruct((3 * n_k, width), bf16),
        ],
        scratch_shapes=[
            pltpu.VMEM((n_k, n_p, n_q), bf16),
            pltpu.VMEM((chunks, n_q, width), bf16),
            pltpu.VMEM((chunks, n_p, width), bf16),
            pltpu.VMEM((chunks, members, rows, width), f32),
            pltpu.VMEM((chunks, members - 1, rows, width), f32),
            pltpu.VMEM((chunks, members, rows, width), f32),
            pltpu.VMEM((members, rows, width), f32),
            pltpu.VMEM((n_k, width), f32),
            pltpu.VMEM((n_k, width), f32),
            dma((n_k // group,)),
            dma((chunks,)),
            dma((chunks,)),
            dma((chunks, n_rep - 1)),
            dma((chunks, members - 1)),
            dma((chunks, members - 1)),
            dma((chunks, members - 1)),
            dma((chunks, members - 1)),
            dma((chunks, n_pts - 1)),
            dma((members,)),
        ],
        compiler_params=pltpu.CompilerParams(
            collective_id=0, has_side_effects=True, vmem_limit_bytes=60 << 20
        ),
        cost_estimate=pl.CostEstimate(
            flops=2 * n_k * n_p * n_q * own_pts,
            bytes_accessed=2 * (n_k * n_p * n_q + (n_p + n_q) * own_pts),
            transcendentals=0,
        ),
    )(density, orbitals)


def outer_kernel(
    scale, tile, slots, left_hbm, right_hbm, o_ref, left, right, buf, in_sem, sem
):
    steps = o_ref.shape[0] // tile
    parts = in_sem.shape[0] - 1
    width = o_ref.shape[0] // parts

    def fetch(g):
        there = pl.ds(g * width, width)
        return pltpu.make_async_copy(left_hbm.at[:, there], left.at[:, there], in_sem.at[g])

    def store(i):
        return pltpu.make_async_copy(
            buf.at[i % slots], o_ref.at[pl.ds(i * tile, tile)], sem.at[i % slots]
        )

    whole = pltpu.make_async_copy(right_hbm, right, in_sem.at[parts])
    whole.start()
    for g in range(parts):
        fetch(g).start()
    whole.wait()
    for i in range(steps):
        if i * tile % width == 0:
            fetch(i * tile // width).wait()
        if i >= slots:
            store(i - slots).wait()
        buf[i % slots] = (
            lax.dot_general(
                left[:, i * tile : (i + 1) * tile], right[...],
                (((0,), (0,)), ((), ())), preferred_element_type=jnp.float32,
            )
            * scale
        )
        store(i).start()
    for i in range(max(0, steps - slots), steps):
        store(i).wait()


def outer(left, right, scale, tile=256, slots=4, parts=4):
    n_rows, n_cols = left.shape[1], right.shape[1]
    tile = min(tile, n_rows // parts)
    return pl.pallas_call(
        functools.partial(outer_kernel, scale, tile, slots),
        in_specs=[pl.BlockSpec(memory_space=pl.ANY)] * 2,
        out_specs=pl.BlockSpec(memory_space=pl.ANY),
        out_shape=jax.ShapeDtypeStruct((n_rows, n_cols), jnp.float32),
        scratch_shapes=[
            pltpu.VMEM(left.shape, left.dtype),
            pltpu.VMEM(right.shape, right.dtype),
            pltpu.VMEM((slots, tile, n_cols), jnp.float32),
            pltpu.SemaphoreType.DMA((parts + 1,)),
            pltpu.SemaphoreType.DMA((slots,)),
        ],
        compiler_params=pltpu.CompilerParams(vmem_limit_bytes=62 << 20),
    )(left, right)


def per_device(density_slab, orbitals):
    left, right = factors(density_slab, orbitals)
    return outer(left, right, 1.0 / density_slab.shape[0])


def solution(mesh):
    return jax.shard_map(
        per_device,
        mesh=mesh,
        in_specs=(P("groups", "aux", "rep"), P(("groups", "rep"), "pts")),
        out_specs=P(("groups", "pts"), ("aux", "rep")),
        check_vma=False,
    )
```

```python
import functools

import jax
import jax.numpy as jnp
from jax import lax
from jax.experimental import pallas as pl
from jax.experimental.pallas import tpu as pltpu
from jax.sharding import PartitionSpec as P


MESH = pl.DeviceIdType.MESH


def split(w):
    high = w.astype(jnp.bfloat16)
    return high, (w - high.astype(jnp.float32)).astype(jnp.bfloat16)


def share_kernel(
    sizes, d_hbm, orb_hbm, left_ref, right_ref,
    d_buf, q_buf, p_buf, part, rs_buf, ag_buf, col_buf, flat, col_flat,
    d_sem, q_sem, p_sem, ps_sem, rs_send, rs_recv, ag_send, ag_recv, col_send, col_recv,
):
    n_aux, n_pts, n_rep, group, tile = sizes
    n_k, n_p, n_q = d_hbm.shape
    members = n_aux * n_rep
    chunks, _, rows, width = part.shape
    a, x, r = lax.axis_index("aux"), lax.axis_index("pts"), lax.axis_index("rep")
    me = a * n_rep + r
    home = me // chunks
    first = a * n_p
    owner, offset = first // n_q, pl.multiple_of(first % n_q, n_p)

    def member(j):
        return {"aux": j // n_rep, "rep": j % n_rep}

    def cols(g):
        return pl.ds(pl.multiple_of(g * width, width), width)

    def d_copy(i):
        ks = pl.ds(i * group, group)
        return pltpu.make_async_copy(d_hbm.at[ks], d_buf.at[ks], d_sem.at[i])

    def q_copy(g):
        return pltpu.make_async_copy(orb_hbm.at[:, cols(g)], q_buf.at[g], q_sem.at[g])

    def p_local(g):
        return pltpu.make_async_copy(
            orb_hbm.at[pl.ds(offset, n_p), cols(g)], p_buf.at[g], p_sem.at[g]
        )

    def p_remote(g, step):
        return pltpu.make_async_remote_copy(
            orb_hbm.at[pl.ds(offset, n_p), cols(g)], p_buf.at[g],
            ps_sem.at[g, step - 1], p_sem.at[g],
            device_id={"rep": (r + step) % n_rep}, device_id_type=MESH,
        )

    def rs_copy(g, step):
        j = (me + step) % members
        return pltpu.make_async_remote_copy(
            part.at[g, j], rs_buf.at[g, step - 1],
            rs_send.at[g, step - 1], rs_recv.at[g, step - 1],
            device_id=member(j), device_id_type=MESH,
        )

    def ag_copy(g, step):
        return pltpu.make_async_remote_copy(
            ag_buf.at[g, me], ag_buf.at[g, me],
            ag_send.at[g, step - 1], ag_recv.at[g, step - 1],
            device_id=member((me + step) % members), device_id_type=MESH,
        )

    def ag_arrival(g, step):
        source = (me + members - step) % members
        return pltpu.make_async_remote_copy(
            ag_buf.at[g, source], ag_buf.at[g, source],
            ag_send.at[g, step - 1], ag_recv.at[g, step - 1],
            device_id=member((me + step) % members), device_id_type=MESH,
        )

    def col_copy(g, step):
        target = member(x * chunks + g)
        target["pts"] = (x + step) % n_pts
        return pltpu.make_async_remote_copy(
            ag_buf.at[g, me], col_buf.at[me],
            col_send.at[g, step - 1], col_recv.at[me],
            device_id=target, device_id_type=MESH,
        )

    def col_arrival(i):
        return pltpu.make_async_remote_copy(
            ag_buf.at[0, i], col_buf.at[i], col_send.at[0, 0], col_recv.at[i],
            device_id={"pts": home}, device_id_type=MESH,
        )

    d_copy(0).start()
    q_copy(0).start()
    for i in range(1, n_k // group):
        d_copy(i).start()
    for g in range(1, chunks):
        q_copy(g).start()

    barrier = pltpu.get_barrier_semaphore()
    for step in range(1, members):
        pl.semaphore_signal(
            barrier, inc=1, device_id=member((me + step) % members), device_id_type=MESH
        )

    @pl.when(home != x)
    def _():
        for i in range(members):
            source = {"aux": i // n_rep, "rep": i % n_rep, "pts": home}
            pl.semaphore_signal(barrier, inc=1, device_id=source, device_id_type=MESH)

    @pl.when(owner == r)
    def _():
        for g in range(chunks):
            p_local(g).start()

    pl.semaphore_wait(barrier, members - 1 + (n_pts - 1) * chunks)

    @pl.when(owner == r)
    def _():
        for g in range(chunks):
            for step in range(1, n_rep):
                p_remote(g, step).start()

    def finish(g):
        for step in range(1, members):
            rs_copy(g, step).wait_recv()
        total = part[g, me]
        for step in range(1, members):
            total = total + rs_buf[g, step - 1]
        ag_buf[g, me] = total
        for step in range(1, members):
            ag_copy(g, step).start()
        for step in range(1, n_pts):
            col_copy(g, step).start()

    def chunk(g, carry):
        q_copy(g).wait()

        @pl.when(g == 0)
        def _():
            for i in range(n_k // group):
                d_copy(i).wait()

        @pl.when(owner == r)
        def _():
            p_local(g).wait()

        @pl.when(owner != r)
        def _():
            p_remote(g, 1).wait_recv()

        for t in range(0, width, tile):
            q_rows = q_buf[g, :, t : t + tile]
            p_rows = p_buf[g, :, t : t + tile].astype(jnp.float32)
            for k in range(0, n_k, group):
                lhs = d_buf[k : k + group].reshape(group * n_p, n_q)
                c = jnp.dot(lhs, q_rows, preferred_element_type=jnp.float32)
                for j in range(group):
                    term = c[j * n_p : (j + 1) * n_p] * p_rows
                    row = (k + j) % rows
                    part[g, (k + j) // rows, row : row + 1, t : t + tile] = jnp.sum(
                        term, axis=0, keepdims=True
                    )
        for step in range(1, members):
            rs_copy(g, step).start()

        @pl.when(g > 0)
        def _():
            finish(g - 1)

        return carry

    def assemble(g):
        for step in range(1, members):
            ag_arrival(g, step).wait_recv()
        for i in range(members):
            flat[i * rows : (i + 1) * rows, :] = ag_buf[g, i]
        high, low = split(flat[...])
        there = slice(g * width, (g + 1) * width)
        left_ref[0:n_k, there] = high
        left_ref[n_k : 2 * n_k, there] = high
        left_ref[2 * n_k : 3 * n_k, there] = low

    def drain(g):
        for step in range(1, members):
            rs_copy(g, step).wait_send()
            ag_copy(g, step).wait_send()
        for step in range(1, n_pts):
            col_copy(g, step).wait_send()

    lax.fori_loop(0, chunks, chunk, 0)
    for g in range(chunks - 1):
        assemble(g)
        drain(g)

    @pl.when(owner == r)
    def _():
        for g in range(chunks):
            for step in range(1, n_rep):
                p_remote(g, step).wait_send()

    finish(chunks - 1)
    assemble(chunks - 1)

    @pl.when(home == x)
    def _():
        for i in range(members):
            col_flat[i * rows : (i + 1) * rows, :] = ag_buf[me % chunks, i]

    @pl.when(home != x)
    def _():
        for i in range(members):
            col_arrival(i).wait_recv()
            col_flat[i * rows : (i + 1) * rows, :] = col_buf[i]

    high, low = split(col_flat[...])
    right_ref[0:n_k, :] = high
    right_ref[n_k : 2 * n_k, :] = low
    right_ref[2 * n_k : 3 * n_k, :] = high
    drain(chunks - 1)


def factors(density, orbitals, group=4, tile=512):
    n_k, n_p, n_q = density.shape
    own_pts = orbitals.shape[1]
    n_aux, n_pts, n_rep = (lax.axis_size(name) for name in ("aux", "pts", "rep"))
    members = n_aux * n_rep
    chunks = members // n_pts
    width = own_pts // chunks
    rows = n_k // members
    dma = pltpu.SemaphoreType.DMA
    f32, bf16 = jnp.float32, jnp.bfloat16
    return pl.pallas_call(
        functools.partial(share_kernel, (n_aux, n_pts, n_rep, group, min(tile, width))),
        in_specs=[pl.BlockSpec(memory_space=pl.ANY)] * 2,
        out_specs=[pl.BlockSpec(memory_space=pltpu.VMEM)] * 2,
        out_shape=[
            jax.ShapeDtypeStruct((3 * n_k, own_pts), bf16),
            jax.ShapeDtypeStruct((3 * n_k, width), bf16),
        ],
        scratch_shapes=[
            pltpu.VMEM((n_k, n_p, n_q), bf16),
            pltpu.VMEM((chunks, n_q, width), bf16),
            pltpu.VMEM((chunks, n_p, width), bf16),
            pltpu.VMEM((chunks, members, rows, width), f32),
            pltpu.VMEM((chunks, members - 1, rows, width), f32),
            pltpu.VMEM((chunks, members, rows, width), f32),
            pltpu.VMEM((members, rows, width), f32),
            pltpu.VMEM((n_k, width), f32),
            pltpu.VMEM((n_k, width), f32),
            dma((n_k // group,)),
            dma((chunks,)),
            dma((chunks,)),
            dma((chunks, n_rep - 1)),
            dma((chunks, members - 1)),
            dma((chunks, members - 1)),
            dma((chunks, members - 1)),
            dma((chunks, members - 1)),
            dma((chunks, n_pts - 1)),
            dma((members,)),
        ],
        compiler_params=pltpu.CompilerParams(
            collective_id=0, has_side_effects=True, vmem_limit_bytes=60 << 20
        ),
        cost_estimate=pl.CostEstimate(
            flops=2 * n_k * n_p * n_q * own_pts,
            bytes_accessed=2 * (n_k * n_p * n_q + (n_p + n_q) * own_pts),
            transcendentals=0,
        ),
    )(density, orbitals)


def outer_kernel(
    scale, tile, slots, left_hbm, right_hbm, o_ref, left, right, buf, in_sem, sem
):
    steps = o_ref.shape[0] // tile
    parts = in_sem.shape[0] - 1
    width = o_ref.shape[0] // parts

    def fetch(g):
        there = pl.ds(g * width, width)
        return pltpu.make_async_copy(left_hbm.at[:, there], left.at[:, there], in_sem.at[g])

    def store(i):
        return pltpu.make_async_copy(
            buf.at[i % slots], o_ref.at[pl.ds(i * tile, tile)], sem.at[i % slots]
        )

    whole = pltpu.make_async_copy(right_hbm, right, in_sem.at[parts])
    whole.start()
    for g in range(parts):
        fetch(g).start()
    whole.wait()
    for i in range(steps):
        if i * tile % width == 0:
            fetch(i * tile // width).wait()
        if i >= slots:
            store(i - slots).wait()
        buf[i % slots] = (
            lax.dot_general(
                left[:, i * tile : (i + 1) * tile], right[...],
                (((0,), (0,)), ((), ())), preferred_element_type=jnp.float32,
            )
            * scale
        )
        store(i).start()
    for i in range(max(0, steps - slots), steps):
        store(i).wait()


def outer(left, right, scale, tile=256, slots=4, parts=4):
    n_rows, n_cols = left.shape[1], right.shape[1]
    tile = min(tile, n_rows // parts)
    return pl.pallas_call(
        functools.partial(outer_kernel, scale, tile, slots),
        in_specs=[pl.BlockSpec(memory_space=pl.ANY)] * 2,
        out_specs=pl.BlockSpec(memory_space=pl.ANY),
        out_shape=jax.ShapeDtypeStruct((n_rows, n_cols), jnp.float32),
        scratch_shapes=[
            pltpu.VMEM(left.shape, left.dtype),
            pltpu.VMEM(right.shape, right.dtype),
            pltpu.VMEM((slots, tile, n_cols), jnp.float32),
            pltpu.SemaphoreType.DMA((parts + 1,)),
            pltpu.SemaphoreType.DMA((slots,)),
        ],
        compiler_params=pltpu.CompilerParams(vmem_limit_bytes=62 << 20),
    )(left, right)


def per_device(density_slab, orbitals):
    left, right = factors(density_slab, orbitals)
    return outer(left, right, 1.0 / density_slab.shape[0])


def solution(mesh):
    return jax.shard_map(
        per_device,
        mesh=mesh,
        in_specs=(P("groups", "aux", "rep"), P(("groups", "rep"), "pts")),
        out_specs=P(("groups", "pts"), ("aux", "rep")),
        check_vma=False,
    )
```

```python
import functools

import jax
import jax.numpy as jnp
from jax import lax
from jax.experimental import pallas as pl
from jax.experimental.pallas import tpu as pltpu
from jax.sharding import PartitionSpec as P


MESH = pl.DeviceIdType.MESH


def split(w):
    high = w.astype(jnp.bfloat16)
    return high, (w - high.astype(jnp.float32)).astype(jnp.bfloat16)


def share_kernel(
    sizes, d_hbm, orb_hbm, left_ref, right_ref,
    d_buf, q_buf, p_buf, part, rs_buf, ag_buf, col_buf, flat, col_flat,
    d_sem, q_sem, p_sem, ps_sem, rs_send, rs_recv, ag_send, ag_recv, col_send, col_recv,
):
    n_aux, n_pts, n_rep, group, tile = sizes
    n_k, n_p, n_q = d_hbm.shape
    members = n_aux * n_rep
    chunks, _, rows, width = part.shape
    a, x, r = lax.axis_index("aux"), lax.axis_index("pts"), lax.axis_index("rep")
    me = a * n_rep + r
    home = me // chunks
    first = a * n_p
    owner, offset = first // n_q, pl.multiple_of(first % n_q, n_p)

    def member(j):
        return {"aux": j // n_rep, "rep": j % n_rep}

    def cols(g):
        return pl.ds(pl.multiple_of(g * width, width), width)

    def d_copy(i):
        ks = pl.ds(i * group, group)
        return pltpu.make_async_copy(d_hbm.at[ks], d_buf.at[ks], d_sem.at[i])

    def q_copy(g):
        return pltpu.make_async_copy(orb_hbm.at[:, cols(g)], q_buf.at[g], q_sem.at[g])

    def p_local(g):
        return pltpu.make_async_copy(
            orb_hbm.at[pl.ds(offset, n_p), cols(g)], p_buf.at[g], p_sem.at[g]
        )

    def p_remote(g, step):
        return pltpu.make_async_remote_copy(
            orb_hbm.at[pl.ds(offset, n_p), cols(g)], p_buf.at[g],
            ps_sem.at[g, step - 1], p_sem.at[g],
            device_id={"rep": (r + step) % n_rep}, device_id_type=MESH,
        )

    def rs_copy(g, step):
        j = (me + step) % members
        return pltpu.make_async_remote_copy(
            part.at[g, j], rs_buf.at[g, step - 1],
            rs_send.at[g, step - 1], rs_recv.at[g, step - 1],
            device_id=member(j), device_id_type=MESH,
        )

    def ag_copy(g, step):
        return pltpu.make_async_remote_copy(
            ag_buf.at[g, me], ag_buf.at[g, me],
            ag_send.at[g, step - 1], ag_recv.at[g, step - 1],
            device_id=member((me + step) % members), device_id_type=MESH,
        )

    def ag_arrival(g, step):
        source = (me + members - step) % members
        return pltpu.make_async_remote_copy(
            ag_buf.at[g, source], ag_buf.at[g, source],
            ag_send.at[g, step - 1], ag_recv.at[g, step - 1],
            device_id=member((me + step) % members), device_id_type=MESH,
        )

    def col_copy(g, step):
        target = member(x * chunks + g)
        target["pts"] = (x + step) % n_pts
        return pltpu.make_async_remote_copy(
            ag_buf.at[g, me], col_buf.at[me],
            col_send.at[g, step - 1], col_recv.at[me],
            device_id=target, device_id_type=MESH,
        )

    def col_arrival(i):
        return pltpu.make_async_remote_copy(
            ag_buf.at[0, i], col_buf.at[i], col_send.at[0, 0], col_recv.at[i],
            device_id={"pts": home}, device_id_type=MESH,
        )

    d_copy(0).start()
    q_copy(0).start()
    for i in range(1, n_k // group):
        d_copy(i).start()
    for g in range(1, chunks):
        q_copy(g).start()

    barrier = pltpu.get_barrier_semaphore()
    for step in range(1, members):
        pl.semaphore_signal(
            barrier, inc=1, device_id=member((me + step) % members), device_id_type=MESH
        )

    @pl.when(home != x)
    def _():
        for i in range(members):
            source = {"aux": i // n_rep, "rep": i % n_rep, "pts": home}
            pl.semaphore_signal(barrier, inc=1, device_id=source, device_id_type=MESH)

    @pl.when(owner == r)
    def _():
        for g in range(chunks):
            p_local(g).start()

    pl.semaphore_wait(barrier, members - 1 + (n_pts - 1) * chunks)

    @pl.when(owner == r)
    def _():
        for g in range(chunks):
            for step in range(1, n_rep):
                p_remote(g, step).start()

    def finish(g):
        for step in range(1, members):
            rs_copy(g, step).wait_recv()
        total = part[g, me]
        for step in range(1, members):
            total = total + rs_buf[g, step - 1]
        ag_buf[g, me] = total
        for step in range(1, members):
            ag_copy(g, step).start()
        for step in range(1, n_pts):
            col_copy(g, step).start()

    def chunk(g, carry):
        q_copy(g).wait()

        @pl.when(g == 0)
        def _():
            for i in range(n_k // group):
                d_copy(i).wait()

        @pl.when(owner == r)
        def _():
            p_local(g).wait()

        @pl.when(owner != r)
        def _():
            p_remote(g, 1).wait_recv()

        for t in range(0, width, tile):
            q_rows = q_buf[g, :, t : t + tile]
            p_rows = p_buf[g, :, t : t + tile].astype(jnp.float32)
            for k in range(0, n_k, group):
                lhs = d_buf[k : k + group].reshape(group * n_p, n_q)
                c = jnp.dot(lhs, q_rows, preferred_element_type=jnp.float32)
                for j in range(group):
                    term = c[j * n_p : (j + 1) * n_p] * p_rows
                    row = (k + j) % rows
                    part[g, (k + j) // rows, row : row + 1, t : t + tile] = jnp.sum(
                        term, axis=0, keepdims=True
                    )
        for step in range(1, members):
            rs_copy(g, step).start()

        @pl.when(g > 0)
        def _():
            finish(g - 1)

        return carry

    def assemble(g):
        for step in range(1, members):
            ag_arrival(g, step).wait_recv()
        for i in range(members):
            flat[i * rows : (i + 1) * rows, :] = ag_buf[g, i]
        high, low = split(flat[...])
        there = slice(g * width, (g + 1) * width)
        left_ref[0:n_k, there] = high
        left_ref[n_k : 2 * n_k, there] = high
        left_ref[2 * n_k : 3 * n_k, there] = low

    def drain(g):
        for step in range(1, members):
            rs_copy(g, step).wait_send()
            ag_copy(g, step).wait_send()
        for step in range(1, n_pts):
            col_copy(g, step).wait_send()

    lax.fori_loop(0, chunks, chunk, 0)
    for g in range(chunks - 2):
        assemble(g)
        drain(g)

    @pl.when(owner == r)
    def _():
        for g in range(chunks):
            for step in range(1, n_rep):
                p_remote(g, step).wait_send()

    finish(chunks - 1)
    for g in range(chunks - 2, chunks):
        assemble(g)

    @pl.when(home == x)
    def _():
        for i in range(members):
            col_flat[i * rows : (i + 1) * rows, :] = ag_buf[me % chunks, i]

    @pl.when(home != x)
    def _():
        for i in range(members):
            col_arrival(i).wait_recv()
            col_flat[i * rows : (i + 1) * rows, :] = col_buf[i]

    high, low = split(col_flat[...])
    right_ref[0:n_k, :] = high
    right_ref[n_k : 2 * n_k, :] = low
    right_ref[2 * n_k : 3 * n_k, :] = high
    for g in range(chunks - 2, chunks):
        drain(g)


def factors(density, orbitals, group=2, tile=1024):
    n_k, n_p, n_q = density.shape
    own_pts = orbitals.shape[1]
    n_aux, n_pts, n_rep = (lax.axis_size(name) for name in ("aux", "pts", "rep"))
    members = n_aux * n_rep
    chunks = members // n_pts
    width = own_pts // chunks
    rows = n_k // members
    dma = pltpu.SemaphoreType.DMA
    f32, bf16 = jnp.float32, jnp.bfloat16
    return pl.pallas_call(
        functools.partial(share_kernel, (n_aux, n_pts, n_rep, group, min(tile, width))),
        in_specs=[pl.BlockSpec(memory_space=pl.ANY)] * 2,
        out_specs=[pl.BlockSpec(memory_space=pltpu.VMEM)] * 2,
        out_shape=[
            jax.ShapeDtypeStruct((3 * n_k, own_pts), bf16),
            jax.ShapeDtypeStruct((3 * n_k, width), bf16),
        ],
        scratch_shapes=[
            pltpu.VMEM((n_k, n_p, n_q), bf16),
            pltpu.VMEM((chunks, n_q, width), bf16),
            pltpu.VMEM((chunks, n_p, width), bf16),
            pltpu.VMEM((chunks, members, rows, width), f32),
            pltpu.VMEM((chunks, members - 1, rows, width), f32),
            pltpu.VMEM((chunks, members, rows, width), f32),
            pltpu.VMEM((members, rows, width), f32),
            pltpu.VMEM((n_k, width), f32),
            pltpu.VMEM((n_k, width), f32),
            dma((n_k // group,)),
            dma((chunks,)),
            dma((chunks,)),
            dma((chunks, n_rep - 1)),
            dma((chunks, members - 1)),
            dma((chunks, members - 1)),
            dma((chunks, members - 1)),
            dma((chunks, members - 1)),
            dma((chunks, n_pts - 1)),
            dma((members,)),
        ],
        compiler_params=pltpu.CompilerParams(
            collective_id=0, has_side_effects=True, vmem_limit_bytes=60 << 20
        ),
        cost_estimate=pl.CostEstimate(
            flops=2 * n_k * n_p * n_q * own_pts,
            bytes_accessed=2 * (n_k * n_p * n_q + (n_p + n_q) * own_pts),
            transcendentals=0,
        ),
    )(density, orbitals)


def outer_kernel(
    scale, tile, slots, left_hbm, right_hbm, o_ref, left, right, buf, in_sem, sem
):
    steps = o_ref.shape[0] // tile
    parts = in_sem.shape[0] - 1
    width = o_ref.shape[0] // parts

    def fetch(g):
        there = pl.ds(g * width, width)
        return pltpu.make_async_copy(left_hbm.at[:, there], left.at[:, there], in_sem.at[g])

    def store(i):
        return pltpu.make_async_copy(
            buf.at[i % slots], o_ref.at[pl.ds(i * tile, tile)], sem.at[i % slots]
        )

    whole = pltpu.make_async_copy(right_hbm, right, in_sem.at[parts])
    whole.start()
    for g in range(parts):
        fetch(g).start()
    whole.wait()
    for i in range(steps):
        if i * tile % width == 0:
            fetch(i * tile // width).wait()
        if i >= slots:
            store(i - slots).wait()
        buf[i % slots] = (
            lax.dot_general(
                left[:, i * tile : (i + 1) * tile], right[...],
                (((0,), (0,)), ((), ())), preferred_element_type=jnp.float32,
            )
            * scale
        )
        store(i).start()
    for i in range(max(0, steps - slots), steps):
        store(i).wait()


def outer(left, right, scale, tile=256, slots=4, parts=4):
    n_rows, n_cols = left.shape[1], right.shape[1]
    tile = min(tile, n_rows // parts)
    return pl.pallas_call(
        functools.partial(outer_kernel, scale, tile, slots),
        in_specs=[pl.BlockSpec(memory_space=pl.ANY)] * 2,
        out_specs=pl.BlockSpec(memory_space=pl.ANY),
        out_shape=jax.ShapeDtypeStruct((n_rows, n_cols), jnp.float32),
        scratch_shapes=[
            pltpu.VMEM(left.shape, left.dtype),
            pltpu.VMEM(right.shape, right.dtype),
            pltpu.VMEM((slots, tile, n_cols), jnp.float32),
            pltpu.SemaphoreType.DMA((parts + 1,)),
            pltpu.SemaphoreType.DMA((slots,)),
        ],
        compiler_params=pltpu.CompilerParams(vmem_limit_bytes=62 << 20),
    )(left, right)


def per_device(density_slab, orbitals):
    left, right = factors(density_slab, orbitals)
    return outer(left, right, 1.0 / density_slab.shape[0])


def solution(mesh):
    return jax.shard_map(
        per_device,
        mesh=mesh,
        in_specs=(P("groups", "aux", "rep"), P(("groups", "rep"), "pts")),
        out_specs=P(("groups", "pts"), ("aux", "rep")),
        check_vma=False,
    )
```
